32 devices in a mesh: groups: 2 (over y), tm: 4 (over z), chan: 2 (over x), sub: 2 (over core).
Axes of the slice: x: 2, y: 2, z: 4, core: 2. Of those that a mesh axis runs over, the one named last changes fastest.
Arguments:
- signal: bfloat16 [2, 240, 65536], P(None, 'chan', ('groups', 'tm', 'sub')), parts along dimension 2, may hold values from -6 to 6
- channel_mask: int32 [240], P('chan'), may hold values from 0 to 1, as said below
- dispersion: float32 [240], P('chan'), may hold values from 1228.8 to 12288
- equaliser: bfloat16 [96, 2, 240, 240], P(('tm', 'chan')), may hold values from -0.25 to 0.25
- bin_block: int32 [64, 128], P(None, ('tm', 'chan')), may hold values from 0 to 11
Outputs:
- output: bfloat16 [2, 240, 65536], P(None, 'chan', ('groups', 'tm', 'sub')), parts along dimension 2
The draws below stay inside these ranges and needn't reach their ends.
There are 2 independent parts, one for each index of `groups`. The reference program is written for one: setup_inputs(seed, part) draws one part's arguments, and reference() takes and returns one part's arrays. A program takes and returns all parts, laid end to end along the dimension named above; an argument that names none is the same for every part. Nothing has to cross between parts.
Inputs may be any that keep to these rules, and one draw needn't show every extreme that they name: `channel_mask`: exactly 228 entries are 1.
All inputs are finite; a program needn't handle non-finite values.
Results may differ from the reference program's by a relative error of at most 0.0089.
Values may be sent and summed in bfloat16 or wider, within the bound.
No kernel may reach another device: no remote copies, remote signals or barrier semaphores. Data moves between devices by JAX's collectives and lax.ppermute only.
A program may use at most 128 MiB of HBM per device.

```python
import math
import jax
import jax.numpy as jnp
from jax import lax

C = 240
VALID = 228
TAPS = 4096
N1 = 128
NB_DEV = 12
NFFT = 8192
N2 = 64
KD = 16
NBLK = 96
TIME = 32768


def draw_channel_mask(key, part):
    order = jax.random.permutation(key, C)
    return jnp.where(order >= C - VALID, 1, 0).astype(jnp.int32)


def set_ends(values, rng, low, high):
    dims = values.shape
    place = [jax.random.randint(jax.random.fold_in(rng, axis), (), 0, dims[axis]) for axis in range(len(dims))]
    values = values.at[tuple(place)].set(low)
    longest = dims.index(max(dims))
    place[longest] = (place[longest] + 1) % dims[longest]
    return values.at[tuple(place)].set(high)


def block_scale(own_key, dims, cuts, low, largest):
    gain, own = 1.0, jax.random.fold_in(own_key, 6)
    for axis_at, shards_of in cuts:
        heights = jnp.exp(jax.random.uniform(jax.random.fold_in(own, axis_at), (shards_of,), jnp.float32, low / len(cuts), largest / len(cuts)))
        gain = gain * jnp.repeat(heights, dims[axis_at] // shards_of).reshape([-1 if axis == axis_at else 1 for axis in range(len(dims))])
    return gain


def gaussian(key, shape, width, limit, pieces=(), held_as=jnp.bfloat16):
    drawn = jax.random.normal(key, shape, jnp.float32) * width
    if len(pieces) > 0:
        drawn = block_scale(key, shape, pieces, -0.22, 0.18) * drawn
    return jnp.clip(drawn, min=-limit, max=limit).astype(held_as)


def setup_inputs(seed: int = 0, part: int = 0) -> dict:
    keys = jax.random.split(jax.random.key(seed), 6)
    part_keys = jax.random.split(jax.random.fold_in(keys[5], part), 6)
    signal = gaussian(part_keys[0], (2, C, TIME), 1.0, 6.0, ((1, 2), (2, 8)))
    channel_mask = draw_channel_mask(jax.random.fold_in(keys[5], 71), part)
    dispersion = jnp.clip(1228.8 + 11059.2 * jax.random.uniform(keys[2], (C,), jnp.float32) ** block_scale(keys[2], (C,), ((0, 2),), -0.2, 0.2), 1228.8, 12288.0)
    equaliser = gaussian(keys[3], (NBLK, 2, C, C), (2 * C) ** -0.5, 0.25, ((0, 8),))
    bin_block = set_ends(jax.random.randint(keys[4], (N2, N1), 0, NB_DEV), jax.random.fold_in(keys[4], 1), 0, NB_DEV - 1).astype(jnp.int32)
    return {"signal": signal, "channel_mask": channel_mask, "dispersion": dispersion, "equaliser": equaliser, "bin_block": bin_block}


def dft_table(length, inverse):
    counter = jnp.arange(length, dtype=jnp.int32)
    product = counter[:, None] * counter[None, :] % length
    angle = product.astype(jnp.float32) * (2.0 * math.pi / length)
    factor = 1.0 / math.sqrt(length)
    cosine = jnp.cos(angle) * factor
    sine = jnp.sin(angle) * factor
    if inverse:
        upper = jnp.stack([cosine, -sine], axis=1)
        lower = jnp.stack([sine, cosine], axis=1)
    else:
        upper = jnp.stack([cosine, sine], axis=1)
        lower = jnp.stack([-sine, cosine], axis=1)
    return jnp.stack([upper, lower], axis=0).astype(jnp.bfloat16)

def twist_table(first_rows, columns):
    seconds = jnp.arange(columns, dtype=jnp.int32)
    product = first_rows[:, None] * seconds[None, :] % NFFT
    angle = product.astype(jnp.float32) * (2.0 * math.pi / NFFT)
    return (jnp.cos(angle), jnp.sin(angle))

def phase_table(dispersion):
    first_rows = jnp.arange(N1, dtype=jnp.int32)
    seconds = jnp.arange(N2, dtype=jnp.int32)
    bins = first_rows[:, None] + N1 * seconds[None, :]
    centred = jnp.where(bins < NFFT // 2, bins, bins - NFFT)
    freq_sq = (centred * centred).astype(jnp.float32) / float(NFFT * NFFT)
    quarter = jnp.mod(centred, 4).astype(jnp.float32) * (0.5 * math.pi)
    phase = dispersion[:, None, None] * freq_sq[None] - quarter[None]
    return (jnp.cos(phase), jnp.sin(phase))

def reference(signal, channel_mask, dispersion, equaliser, bin_block):
    mask_half = channel_mask.astype(jnp.bfloat16)
    masked = signal * mask_half[None, :, None]
    frame_count = TIME // TAPS
    padded = jnp.concatenate([jnp.zeros((2, C, TAPS), jnp.bfloat16), masked], axis=2)
    halves = padded.reshape(2, C, frame_count + 1, TAPS)
    frames = jnp.concatenate([halves[:, :, :-1], halves[:, :, 1:]], axis=3)
    forward_first = dft_table(N1, False).astype(jnp.float32)
    forward_second = dft_table(N2, False).astype(jnp.float32)
    inverse_first = dft_table(N1, True).astype(jnp.float32)
    inverse_second = dft_table(N2, True).astype(jnp.float32)
    cos_twist, sin_twist = twist_table(jnp.arange(N1, dtype=jnp.int32), N2)
    cos_disp, sin_disp = phase_table(dispersion)

    def forward(frame):
        shaped = frame.reshape(2, C, N1, N2).astype(jnp.float32)
        section_a = jnp.einsum('pkqt,qcts->cpks', forward_first, shaped)
        real_a = section_a[:, 0]
        imag_a = section_a[:, 1]
        twisted = jnp.stack([real_a * cos_twist + imag_a * sin_twist, imag_a * cos_twist - real_a * sin_twist], axis=1).astype(jnp.bfloat16)
        spectrum = jnp.einsum('rlps,cpks->ckrl', forward_second, twisted.astype(jnp.float32))
        real_s = spectrum[:, :, 0]
        imag_s = spectrum[:, :, 1]
        dispersed = jnp.stack([real_s * cos_disp - imag_s * sin_disp, real_s * sin_disp + imag_s * cos_disp], axis=2)
        return dispersed.astype(jnp.bfloat16)
    spectra = lax.map(forward, jnp.moveaxis(frames, 2, 0))
    groups_of = jnp.arange(N1, dtype=jnp.int32) // KD * NB_DEV
    blocks = groups_of[None, :] + bin_block

    def equalise(inputs):
        columns, picks = inputs
        chosen = jnp.take(equaliser, picks, axis=0).astype(jnp.float32)
        mixed = jnp.einsum('jsoc,mcjq->mojsq', chosen, columns.astype(jnp.float32))
        real_e = mixed[..., 0, 0] - mixed[..., 1, 1]
        imag_e = mixed[..., 0, 1] + mixed[..., 1, 0]
        return jnp.stack([real_e, imag_e], axis=-1).astype(jnp.bfloat16)
    equalised = lax.map(equalise, (jnp.moveaxis(spectra, 4, 0), blocks))
    equalised = jnp.transpose(equalised, (1, 2, 3, 4, 0))

    def inverse(spectrum):
        partial_value = jnp.einsum('rtpk,cjpk->crjt', inverse_second, spectrum.astype(jnp.float32))
        real_g = partial_value[:, 0]
        imag_g = partial_value[:, 1]
        turned = jnp.stack([real_g * cos_twist - imag_g * sin_twist, imag_g * cos_twist + real_g * sin_twist], axis=1).astype(jnp.bfloat16)
        values = jnp.einsum('rupj,cpjt->rcut', inverse_first[:, N1 // 2:], turned.astype(jnp.float32))
        return values.reshape(2, C, TAPS)
    outputs = lax.map(inverse, equalised)
    result = jnp.moveaxis(outputs, 0, 2).reshape(2, C, TIME)
    return (result * channel_mask.astype(jnp.float32)[None, :, None]).astype(jnp.bfloat16)
```

```python
import functools
import math

import jax
import jax.numpy as jnp
from jax import lax
from jax.experimental import pallas as pl
from jax.experimental.pallas import tpu as pltpu
from jax.sharding import PartitionSpec as P

TAPS = 4096
N1 = 128
NFFT = 8192
N2 = 64
LANES = 2 * N2
BLOCK = 8
QUARTERS = 4


def from_behind(value, axis, by):
    devices = lax.axis_size(axis)
    pairs = [(i, i + by) for i in range(devices) if 0 <= i + by < devices]
    return lax.ppermute(value, axis, pairs)


def cos_sin(rows, columns, length):
    product = rows[:, None] * columns[None, :] % length
    angle = product.astype(jnp.float32) * (2.0 * math.pi / length)
    factor = 1.0 / math.sqrt(length)
    return jnp.cos(angle) * factor, jnp.sin(angle) * factor


def dft_table(length, inverse):
    counter = jnp.arange(length, dtype=jnp.int32)
    cosine, sine = cos_sin(counter, counter, length)
    if inverse:
        upper = jnp.stack([cosine, -sine], axis=1)
        lower = jnp.stack([sine, cosine], axis=1)
    else:
        upper = jnp.stack([cosine, sine], axis=1)
        lower = jnp.stack([-sine, cosine], axis=1)
    return jnp.stack([upper, lower], axis=0).astype(jnp.bfloat16)


def twist_table(first_rows, columns):
    seconds = jnp.arange(columns, dtype=jnp.int32)
    product = first_rows[:, None] * seconds[None, :] % NFFT
    angle = product.astype(jnp.float32) * (2.0 * math.pi / NFFT)
    return (jnp.cos(angle), jnp.sin(angle))


def low_half():
    return lax.broadcasted_iota(jnp.int32, (BLOCK, LANES), 1) < N2


def swap_halves(value):
    return pltpu.roll(value, N2, 1)


def forward_kernel(
    tail, own, first, twist_cos, twist_sin, second, chirp, *refs, slots, rows
):
    outs, (spread, mixed) = refs[:slots], refs[slots:]
    low = low_half()
    half_tiles = TAPS // LANES
    for tile in range(2 * half_tiles):
        source = tail if tile < half_tiles else own
        at = (tile % half_tiles) * LANES
        real = source[0, :, at : at + LANES].astype(jnp.float32)
        imag = source[1, :, at : at + LANES].astype(jnp.float32)
        real_r = swap_halves(real)
        imag_r = swap_halves(imag)
        even = 2 * tile
        spread[pl.ds(even, BLOCK, stride=2 * N1), :] = jnp.where(low, real, imag_r)
        spread[pl.ds(even + 1, BLOCK, stride=2 * N1), :] = jnp.where(low, real_r, imag)
        spread[pl.ds(N1 + even, BLOCK, stride=2 * N1), :] = jnp.where(low, imag, -real_r)
        spread[pl.ds(N1 + even + 1, BLOCK, stride=2 * N1), :] = jnp.where(low, imag_r, -real)
    table = first[...]
    cosine = twist_cos[...]
    sine = twist_sin[...]
    count = slots * rows
    for pair in range(BLOCK // 2):
        at = 4 * N1 * pair
        both = jnp.concatenate(
            [
                spread[at : at + 2 * N1, :].astype(jnp.bfloat16),
                spread[at + 2 * N1 : at + 4 * N1, :].astype(jnp.bfloat16),
            ],
            axis=1,
        )
        section = jnp.dot(table, both, preferred_element_type=jnp.float32)
        for side in range(2):
            part = section[:, side * LANES : (side + 1) * LANES]
            part = part * cosine + swap_halves(part) * sine
            mixed[pl.ds(2 * pair + side, count, stride=BLOCK), :] = part
    spectrum = jnp.dot(
        mixed[...].astype(jnp.bfloat16), second[...], preferred_element_type=jnp.float32
    )
    step_c = chirp[4 * slots]
    step_s = chirp[4 * slots + 1]
    for slot in range(slots):
        turn_c, turn_s, move_c, move_s = (chirp[4 * slot + i] for i in range(4))
        for row in range(rows):
            at = (slot * rows + row) * BLOCK
            part = spectrum[at : at + BLOCK]
            part = part * turn_c + swap_halves(part) * turn_s
            outs[slot][row] = part.astype(jnp.bfloat16)
            if row + 1 < rows:
                turn_c, turn_s = (
                    turn_c * move_c - turn_s * move_s,
                    turn_s * move_c + turn_c * move_s,
                )
                move_c, move_s = (
                    move_c * step_c - move_s * step_s,
                    move_s * step_c + move_c * step_s,
                )


def forward(tail, own, tables, chirp, slots, rows):
    channels = own.shape[1]
    first, twist_cos, twist_sin, second = tables
    whole = lambda a: pl.BlockSpec(a.shape, lambda i: (0,) * a.ndim)
    samples = pl.BlockSpec((2, BLOCK, TAPS), lambda i: (0, i, 0))
    return pl.pallas_call(
        functools.partial(forward_kernel, slots=slots, rows=rows),
        grid=(channels // BLOCK,),
        in_specs=[
            samples,
            samples,
            whole(first),
            whole(twist_cos),
            whole(twist_sin),
            whole(second),
            pl.BlockSpec((chirp.shape[0], BLOCK, LANES), lambda i: (0, i, 0)),
        ],
        out_specs=[pl.BlockSpec((rows, BLOCK, LANES), lambda i: (0, i, 0))] * slots,
        out_shape=[jax.ShapeDtypeStruct((rows, channels, LANES), jnp.bfloat16)] * slots,
        scratch_shapes=[
            pltpu.VMEM((BLOCK * 2 * N1, LANES), jnp.float32),
            pltpu.VMEM((slots * rows * BLOCK, LANES), jnp.float32),
        ],
        name="forward",
    )(tail, own, first, twist_cos, twist_sin, second, chirp)


def equalise_kernel(
    scalars, w0, w1, w2, w3, picks, near, far, second, turn_cos, turn_sin, keep, send,
    columns, total, *, blocks, channels
):
    first_side = scalars[0] == 0
    quarter = scalars[1]
    per = blocks // QUARTERS
    all_channels = 2 * channels
    for side in range(2):
        mine = near[side].astype(jnp.float32)
        other = far[side].astype(jnp.float32)
        lanes = slice(side * LANES, (side + 1) * LANES)
        columns[0:channels, lanes] = jnp.where(first_side, mine, other)
        columns[channels:all_channels, lanes] = jnp.where(first_side, other, mine)
    value = columns[...].astype(jnp.bfloat16)
    pair = pl.program_id(0)
    table = picks[:, 0:LANES].astype(jnp.float32)
    index = lax.broadcasted_iota(jnp.int32, table.shape, 0)
    chosen = jnp.concatenate(
        [
            jnp.sum(jnp.where(index == 2 * pair + side, table, 0.0), axis=0, keepdims=True)
            for side in range(2)
        ],
        axis=1,
    )
    for place in range(QUARTERS):
        weights = (w0, w1, w2, w3)[place]
        owner = jnp.bitwise_xor(quarter, place)
        for item in range(per):
            name = (owner * per + item).astype(jnp.float32)
            mask = jnp.where(chosen == name, 1.0, 0.0).astype(jnp.bfloat16)
            block = weights[item * 2 * all_channels : (item + 1) * 2 * all_channels, :]
            product = jnp.dot(block, value * mask, preferred_element_type=jnp.float32)
            if place == 0 and item == 0:
                total[...] = product
            else:
                total[...] += product
    low = lax.broadcasted_iota(jnp.int32, (1, LANES), 1) < N2
    sign = jnp.where(low, -1.0, 1.0)
    table = second[...]
    for side in range(2):
        lanes = slice(side * LANES, (side + 1) * LANES)
        mixed = total[0:all_channels, lanes] + sign * swap_halves(
            total[all_channels : 2 * all_channels, lanes]
        )
        partial = jnp.dot(
            mixed.astype(jnp.bfloat16), table, preferred_element_type=jnp.float32
        )
        turned = partial * turn_cos[side] + swap_halves(partial) * turn_sin[side]
        lower = turned[0:channels]
        upper = turned[channels:all_channels]
        keep[side] = jnp.where(first_side, lower, upper).astype(jnp.bfloat16)
        send[side] = jnp.where(first_side, upper, lower).astype(jnp.bfloat16)


def equalise(scalars, weights, places, picks, picks_at, near, far, second, turn_cos, turn_sin, blocks):
    rows, channels, _ = near.shape
    per = blocks // QUARTERS
    height = per * 4 * channels
    width = 2 * channels
    pairs = pl.BlockSpec((2, channels, LANES), lambda i, s: (i, 0, 0))
    turn = pl.BlockSpec((2, 1, LANES), lambda i, s: (i, 0, 0))
    fixed = pl.Buffered(1)
    return pl.pallas_call(
        functools.partial(equalise_kernel, blocks=blocks, channels=channels),
        grid_spec=pltpu.PrefetchScalarGridSpec(
            num_scalar_prefetch=1,
            grid=(rows // 2,),
            in_specs=[
                pl.BlockSpec((height, width), lambda i, s, j=j: (j, 0), pipeline_mode=fixed)
                for j in places
            ]
            + [
                pl.BlockSpec((rows, width), lambda i, s: (picks_at, 0), pipeline_mode=fixed),
                pairs,
                pairs,
                pl.BlockSpec((LANES, LANES), lambda i, s: (0, 0)),
                turn,
                turn,
            ],
            out_specs=[pairs, pairs],
            scratch_shapes=[
                pltpu.VMEM((2 * channels, 2 * LANES), jnp.float32),
                pltpu.VMEM((4 * channels, 2 * LANES), jnp.float32),
            ],
        ),
        out_shape=[jax.ShapeDtypeStruct(near.shape, jnp.bfloat16)] * 2,
        name="equalise",
    )(scalars, *weights, picks, near, far, second, turn_cos, turn_sin)


def backward_kernel(*refs, parts, rows):
    ins, (last, mask, out, spread, mixed) = refs[:parts], refs[parts:]
    low = low_half()
    for part in range(parts):
        for row in range(rows):
            value = ins[part][row].astype(jnp.float32)
            at = part * rows + row
            spread[pl.ds(at, BLOCK, stride=2 * N1), :] = value
            turned = swap_halves(value)
            spread[pl.ds(N1 + at, BLOCK, stride=2 * N1), :] = jnp.where(low, -turned, turned)
    table = last[...]
    half = N1 // 2
    for pair in range(BLOCK // 2):
        at = 4 * N1 * pair
        both = jnp.concatenate(
            [
                spread[at : at + 2 * N1, :].astype(jnp.bfloat16),
                spread[at + 2 * N1 : at + 4 * N1, :].astype(jnp.bfloat16),
            ],
            axis=1,
        )
        value = jnp.dot(table, both, preferred_element_type=jnp.float32)
        for side in range(2):
            mixed[pl.ds(2 * pair + side, half, stride=BLOCK), :] = value[
                :, side * LANES : (side + 1) * LANES
            ]
    scale = mask[...]
    for tile in range(half // 2):
        even = mixed[2 * tile * BLOCK : (2 * tile + 1) * BLOCK, :]
        odd = mixed[(2 * tile + 1) * BLOCK : (2 * tile + 2) * BLOCK, :]
        at = slice(tile * LANES, (tile + 1) * LANES)
        real = jnp.where(low, even, swap_halves(odd)) * scale
        imag = jnp.where(low, swap_halves(even), odd) * scale
        out[0, :, at] = real.astype(jnp.bfloat16)
        out[1, :, at] = imag.astype(jnp.bfloat16)


def backward(parts, last, mask):
    rows, channels, _ = parts[0].shape
    return pl.pallas_call(
        functools.partial(backward_kernel, parts=len(parts), rows=rows),
        grid=(channels // BLOCK,),
        in_specs=[pl.BlockSpec((rows, BLOCK, LANES), lambda i: (0, i, 0))] * len(parts)
        + [
            pl.BlockSpec(last.shape, lambda i: (0, 0)),
            pl.BlockSpec((BLOCK, LANES), lambda i: (i, 0)),
        ],
        out_specs=pl.BlockSpec((2, BLOCK, TAPS), lambda i: (0, i, 0)),
        out_shape=jax.ShapeDtypeStruct((2, channels, TAPS), jnp.bfloat16),
        scratch_shapes=[
            pltpu.VMEM((BLOCK * 2 * N1, LANES), jnp.float32),
            pltpu.VMEM((N1 // 2 * BLOCK, LANES), jnp.float32),
        ],
        name="backward",
    )(*parts, last, mask)


def both(value):
    return jnp.concatenate([value, value], axis=-1)


def signed(value, first):
    return jnp.concatenate([first * value, -first * value], axis=-1)


def chirp_table(dispersion, mask, bases, rows):
    seconds = jnp.arange(N2, dtype=jnp.int32)
    base = bases[:, None] + N1 * seconds[None, :]
    centred = jnp.where(base < NFFT // 2, base, base - NFFT)
    whole = float(NFFT * NFFT)
    start = (centred * centred).astype(jnp.float32) / whole
    quarter = jnp.mod(centred, 4).astype(jnp.float32) * (0.5 * math.pi)
    change = (2 * centred + 1).astype(jnp.float32) / whole
    phase = dispersion[None, :, None] * start[:, None] - quarter[:, None]
    move = dispersion[None, :, None] * change[:, None] - 0.5 * math.pi
    scale = mask[None, :, None]
    slots = jnp.stack(
        [
            both(jnp.cos(phase) * scale),
            signed(jnp.sin(phase) * scale, -1.0),
            both(jnp.cos(move)),
            signed(jnp.sin(move), -1.0),
        ],
        axis=1,
    )
    step = jnp.broadcast_to(dispersion[:, None] * (2.0 / whole), (dispersion.shape[0], N2))
    step = jnp.stack([both(jnp.cos(step)), signed(jnp.sin(step), -1.0)])
    return jnp.concatenate([slots.reshape((-1,) + slots.shape[2:]), step])


def second_table(inverse):
    counter = jnp.arange(N2, dtype=jnp.int32)
    cosine, sine = cos_sin(counter, counter, N2)
    sine = -sine if inverse else sine
    upper = jnp.concatenate([cosine, -sine], axis=1)
    lower = jnp.concatenate([sine, cosine], axis=1)
    return jnp.concatenate([upper, lower], axis=0).astype(jnp.bfloat16)


def near_blocks(signal, channel_mask, dispersion, equaliser, bin_block):
    channels = signal.shape[1]
    blocks = equaliser.shape[0]
    tm = lax.axis_size("tm")
    chan = lax.axis_size("chan")
    subs = lax.axis_size("sub")
    rows = N1 // (tm * chan)
    z = lax.axis_index("tm")
    x = lax.axis_index("chan")
    quarter = lax.axis_index("groups") * subs + lax.axis_index("sub")
    per = blocks // QUARTERS
    width = 2 * channels

    tail = from_behind(signal, ("tm", "sub"), 1)

    picks = jnp.transpose(bin_block).astype(jnp.bfloat16)
    picks = jnp.concatenate(
        [picks, picks, jnp.zeros((rows, width - LANES), jnp.bfloat16)], axis=1
    )
    own_part = lax.dynamic_slice_in_dim(equaliser, quarter * per, per, 0)
    own_part = jnp.concatenate([own_part.reshape(per * 2 * width, width), picks], axis=0)
    swap = [(0, 1), (1, 0)]
    weights = {0: [equaliser.reshape(blocks * 2 * width, width)] * QUARTERS}
    for step in (1, tm - 1, *range(2, tm - 1)):
        got = lax.ppermute(own_part, "tm", [(i, (i + step) % tm) for i in range(tm)])
        across = lax.ppermute(got, "groups", swap)
        weights[step] = [
            got,
            lax.ppermute(got, "sub", swap),
            across,
            lax.ppermute(across, "sub", swap),
        ]
    order = [0, 1, tm - 1, *range(2, tm - 1)]
    row = jnp.arange(rows, dtype=jnp.int32)
    bases = jnp.mod(z - jnp.array(order, jnp.int32), tm) * chan
    own_bases = (bases + x) * rows
    other_bases = (bases + (1 - x)) * rows
    own_rows = (own_bases[:, None] + row[None]).reshape(-1)
    other_rows = (other_bases[:, None] + row[None]).reshape(-1)

    firsts = jnp.arange(N1, dtype=jnp.int32)
    second = second_table(False)

    def forward_tables(k1):
        table = jnp.concatenate(cos_sin(k1, firsts, N1), axis=1).astype(jnp.bfloat16)
        cosine, sine = twist_table(k1, N2)
        return table, both(cosine), signed(sine, 1.0), second

    mask = channel_mask.astype(jnp.float32)
    send = forward(
        tail, signal, forward_tables(other_rows),
        chirp_table(dispersion, mask, other_bases, rows), tm, rows,
    )
    keep = forward(
        tail, signal, forward_tables(own_rows),
        chirp_table(dispersion, mask, own_bases, rows), tm, rows,
    )
    got = [lax.ppermute(part, "chan", swap) for part in send]

    inverse = second_table(True)
    cosine, sine = twist_table(own_rows, N2)
    turn_cos = both(cosine).reshape(tm, rows, 1, LANES)
    turn_sin = signed(sine, -1.0).reshape(tm, rows, 1, LANES)
    mine, theirs = [], []
    for slot, step in enumerate(order):
        local = step == 0
        scalars = jnp.stack([x, jnp.zeros_like(quarter) if local else quarter])
        kept, sent = equalise(
            scalars,
            weights[step],
            range(QUARTERS) if local else [0] * QUARTERS,
            picks if local else weights[step][0],
            0 if local else per * 2 * width // rows,
            keep[slot],
            got[slot],
            inverse,
            turn_cos[slot],
            turn_sin[slot],
            blocks,
        )
        mine.append(kept)
        theirs.append(lax.ppermute(sent, "chan", swap))

    last = jnp.concatenate(
        cos_sin(firsts[N1 // 2 :], jnp.concatenate([own_rows, other_rows]), N1), axis=1
    ).astype(jnp.bfloat16)
    spread_mask = jnp.broadcast_to(mask[:, None], (channels, LANES))
    return backward(mine + theirs, last, spread_mask)


def invert_second(spectra, first_rows, inverse_second):
    partial_value = jnp.einsum(
        "rspk,cjfpk->cjfrs", inverse_second, spectra, preferred_element_type=jnp.float32
    )
    cos_inv, sin_inv = twist_table(first_rows, N2)
    cos_inv = cos_inv[:, None, :]
    sin_inv = sin_inv[:, None, :]
    real_g = partial_value[:, :, :, 0]
    imag_g = partial_value[:, :, :, 1]
    turned = jnp.stack(
        [real_g * cos_inv - imag_g * sin_inv, imag_g * cos_inv + real_g * sin_inv], axis=3
    )
    return turned.astype(jnp.bfloat16)


def phase_table(dispersion):
    first_rows = jnp.arange(N1, dtype=jnp.int32)
    seconds = jnp.arange(N2, dtype=jnp.int32)
    bins = first_rows[:, None] + N1 * seconds[None, :]
    centred = jnp.where(bins < NFFT // 2, bins, bins - NFFT)
    freq_sq = (centred * centred).astype(jnp.float32) / float(NFFT * NFFT)
    quarter = jnp.mod(centred, 4).astype(jnp.float32) * (0.5 * math.pi)
    phase = dispersion[:, None, None] * freq_sq[None] - quarter[None]
    return (jnp.cos(phase), jnp.sin(phase))


def far_blocks(signal, channel_mask, dispersion, equaliser, bin_block):
    channels_dev = signal.shape[1]
    frame_count = signal.shape[2] // TAPS
    half_rows = N1 // 2
    mask_half = channel_mask.astype(jnp.bfloat16)
    masked = signal * mask_half[None, :, None]
    tail_in = from_behind(masked, ("tm", "sub"), 1)
    forward_first = dft_table(N1, False)
    forward_second = dft_table(N2, False)
    inverse_first = dft_table(N1, True)
    inverse_second = dft_table(N2, True)
    own_halves = masked.reshape(2, channels_dev, frame_count, TAPS)
    previous = jnp.concatenate([tail_in[:, :, None], own_halves[:, :, :-1]], axis=2)
    frames = jnp.concatenate([previous, own_halves], axis=3).reshape(
        2, channels_dev, frame_count, N1, N2
    )
    section_a = jnp.einsum(
        "pkqt,qcfts->cfpks", forward_first, frames, preferred_element_type=jnp.float32
    )
    cos_twist, sin_twist = twist_table(jnp.arange(N1, dtype=jnp.int32), N2)
    real_a = section_a[:, :, 0]
    imag_a = section_a[:, :, 1]
    twisted = jnp.stack(
        [real_a * cos_twist + imag_a * sin_twist, imag_a * cos_twist - real_a * sin_twist], axis=2
    ).astype(jnp.bfloat16)
    spectrum = jnp.einsum(
        "rlps,cfpks->ckfrl", forward_second, twisted, preferred_element_type=jnp.float32
    )
    cos_disp, sin_disp = phase_table(dispersion)
    cos_disp = cos_disp[:, :, None, :]
    sin_disp = sin_disp[:, :, None, :]
    real_s = spectrum[:, :, :, 0]
    imag_s = spectrum[:, :, :, 1]
    dispersed = jnp.stack(
        [real_s * cos_disp - imag_s * sin_disp, real_s * sin_disp + imag_s * cos_disp], axis=3
    )
    dispersed = dispersed.astype(jnp.bfloat16).reshape(channels_dev, N1, frame_count, 2 * N2)
    by_bins = lax.all_to_all(dispersed, ("tm", "chan"), split_axis=1, concat_axis=1, tiled=True)
    tm_count = lax.axis_size("tm")
    chan_count = lax.axis_size("chan")
    bins_rows = N1 // (tm_count * chan_count)
    grid = by_bins.reshape(channels_dev, tm_count, chan_count, bins_rows, frame_count, 2, N2)
    shaped_weights = equaliser.reshape(
        equaliser.shape[0], 2, chan_count, channels_dev, chan_count, channels_dev
    )
    group_size = 8

    def equalise_group(group_step, result):
        start = group_step * group_size
        columns = lax.dynamic_slice_in_dim(grid, start, group_size, 6)
        picks = lax.dynamic_slice_in_dim(bin_block, start, group_size, 0)
        chosen = jnp.take(shaped_weights, picks, axis=0)
        mixed = jnp.einsum(
            "gjsxyad,dtajfqg->ytxjfsqg", chosen, columns, preferred_element_type=jnp.float32
        )
        real_e = mixed[:, :, :, :, :, 0, 0] - mixed[:, :, :, :, :, 1, 1]
        imag_e = mixed[:, :, :, :, :, 0, 1] + mixed[:, :, :, :, :, 1, 0]
        block_out = jnp.stack([real_e, imag_e], axis=5).astype(jnp.bfloat16)
        return lax.dynamic_update_slice_in_dim(result, block_out, start, 6)

    equalised = lax.fori_loop(
        0, N2 // group_size, equalise_group, jnp.zeros(grid.shape, jnp.bfloat16)
    )
    equalised = equalised.reshape(channels_dev, N1, frame_count, 2, N2)
    returned = lax.all_to_all(
        equalised.reshape(channels_dev, N1, frame_count, 2 * N2),
        ("tm", "chan"),
        split_axis=1,
        concat_axis=1,
        tiled=True,
    )
    returned = returned.reshape(channels_dev, N1, frame_count, 2, N2)
    restored = invert_second(returned, jnp.arange(N1, dtype=jnp.int32), inverse_second)
    values = jnp.einsum(
        "rupj,cjfpt->rcfut",
        inverse_first[:, half_rows:],
        restored,
        preferred_element_type=jnp.float32,
    )
    values = values.reshape(2, channels_dev, frame_count * TAPS)
    return (values * channel_mask.astype(jnp.float32)[None, :, None]).astype(jnp.bfloat16)


def on_device(signal, channel_mask, dispersion, equaliser, bin_block):
    tm = lax.axis_size("tm")
    chan = lax.axis_size("chan")
    sharers = lax.axis_size("groups") * lax.axis_size("sub")
    rows = N1 // (tm * chan)
    fits = (
        chan == 2
        and 2 <= tm <= 4
        and sharers == QUARTERS
        and equaliser.shape[0] % QUARTERS == 0
        and rows % 16 == 0
        and signal.shape[2] == TAPS
        and signal.shape[1] % BLOCK == 0
    )
    plan = near_blocks if fits else far_blocks
    return plan(signal, channel_mask, dispersion, equaliser, bin_block)


def solution(mesh):
    in_specs = (
        P(None, "chan", ("groups", "tm", "sub")),
        P("chan"),
        P("chan"),
        P(("tm", "chan"), None, None, None),
        P(None, ("tm", "chan")),
    )
    out_specs = P(None, "chan", ("groups", "tm", "sub"))
    return jax.shard_map(
        on_device, mesh=mesh, in_specs=in_specs, out_specs=out_specs, check_vma=False
    )
```
